512 devices in a mesh: row: 16 (over y, core), col: 32 (over z, x).
Axes of the slice: x: 4, y: 8, z: 8, core: 2. Of those that a mesh axis runs over, the one named last changes fastest.
Arguments:
- particles: float32 [16384, 128], P('row'), may hold values from -4 to 4
- log_weights: float32 [16384], P('row'), may hold values from -8 to 8
- targets: float32 [49152, 128], P('col'), may hold values from -5 to 5
Outputs:
- new_particles: float32 [49152, 128], P(('col', 'row'))
The draws below stay inside these ranges and needn't reach their ends.
All inputs are finite; a program needn't handle non-finite values.
Results may differ from the reference program's by a relative error of at most 0.005.
Values sent between devices are 32-bit elements; how exact they have to be, the bound alone decides.
No kernel may reach another device: no remote copies, remote signals or barrier semaphores. Data moves between devices by JAX's collectives and lax.ppermute only.
A program may use at most 64 MiB of HBM per device.

```python
import math
import jax
import jax.numpy as jnp
from jax import lax

S = 128
ITERS = 3
N = 16384
M = 49152


def draw_particles(key, part):
    third = jax.random.fold_in(jax.random.fold_in(key, 11), 2)
    return jnp.clip(jax.random.normal(third, (N, S), jnp.float32), -4.0, 4.0)


def draw_targets(key, part):
    third = jax.random.fold_in(jax.random.fold_in(key, 23), 2)
    return jnp.clip(jax.random.normal(third, (M, S), jnp.float32), -5.0, 5.0)


def block_scale(rng, dims, shards, low, top_value):
    def one(position, parts):
        steps = jax.random.uniform(jax.random.fold_in(jax.random.fold_in(rng, 6), position), (parts,), jnp.float32, low / len(shards), top_value / len(shards))
        return jnp.repeat(jnp.exp(steps), dims[position] // parts).reshape((-1,) + (1,) * (len(dims) - position - 1))

    factor_of = one(*shards[0])
    for cut in shards[1:]:
        factor_of = factor_of * one(*cut)
    return factor_of


def centred(key, extent, deviation, limit, cuts=(), held_as=jnp.bfloat16):
    values = deviation * jax.random.normal(key, extent, jnp.float32)
    if cuts:
        values = values * block_scale(key, extent, cuts, -0.22, 0.18)
    return jnp.clip(values, -limit, limit).astype(held_as)


def setup_inputs(seed: int = 0) -> dict:
    key_list = jax.random.split(jax.random.key(seed), 4)
    return {
        "particles": draw_particles(jax.random.fold_in(key_list[3], 71), 0),
        "log_weights": centred(key_list[1], (N,), 2.0, 8.0, ((0, 16),), jnp.float32),
        "targets": draw_targets(jax.random.fold_in(key_list[3], 71), 0),
    }


EPS = 0.01


def cost_tile(source, points):
    source_sq = jnp.sum(source * source, axis=1)
    points_sq = jnp.sum(points * points, axis=1)
    cross = jnp.dot(source, points.T, precision=lax.Precision.HIGHEST, preferred_element_type=jnp.float32)
    return (source_sq[:, None] + points_sq[None, :] - 2.0 * cross) / source.shape[1]


def reference(particles, log_weights, targets):
    total = particles.shape[0]
    block_rows = math.gcd(total, 1024)
    block_count = total // block_rows
    stacked = particles.reshape(block_count, block_rows, particles.shape[1])
    weights_stacked = log_weights.reshape(block_count, block_rows)
    log_count = math.log(targets.shape[0])
    width = targets.shape[0]
    col_pot = jnp.zeros((width,), jnp.float32)
    col_lse = jnp.zeros((width,), jnp.float32)
    for iteration in range(ITERS):
        def row_fn(pair):
            source, weights = pair
            scores = (col_pot[None, :] - cost_tile(source, targets)) / EPS
            top = jnp.max(scores, axis=1)
            summed = jnp.sum(jnp.exp(scores - top[:, None]), axis=1)
            return EPS * (weights - (top + jnp.log(summed)))

        row_pot = lax.map(row_fn, (stacked, weights_stacked))

        def col_fn(carry, pair):
            top_old, sum_old = carry
            source, potential = pair
            scores = (potential[:, None] - cost_tile(source, targets)) / EPS
            top = jnp.maximum(top_old, jnp.max(scores, axis=0))
            summed = sum_old * jnp.exp(top_old - top) + jnp.sum(jnp.exp(scores - top[None, :]), axis=0)
            return (top, summed), None

        start = (jnp.full((width,), -1e30, jnp.float32), jnp.zeros((width,), jnp.float32))
        (top, summed), unused = lax.scan(col_fn, start, (stacked, row_pot))
        col_lse = top + jnp.log(summed)
        col_pot = EPS * (-log_count - col_lse)

    def move_fn(acc, pair):
        source, potential = pair
        plan = jnp.exp((potential[:, None] - cost_tile(source, targets)) / EPS - col_lse[None, :]).astype(jnp.bfloat16)
        moved = lax.dot_general(plan, source.astype(jnp.bfloat16), (((0,), (0,)), ((), ())), preferred_element_type=jnp.float32)
        return acc + moved, None

    result, unused = lax.scan(move_fn, jnp.zeros((width, particles.shape[1]), jnp.float32), (stacked, row_pot))
    return result
```

```python
import math

import jax
import jax.numpy as jnp
from jax import lax
from jax.experimental import pallas as pl
from jax.experimental.pallas import tpu as pltpu
from jax.sharding import PartitionSpec as P

ITERS = 3
EPS = 0.01
LOG2E = math.log2(math.e)
LANES = 128
SUBS = 8
VMEM = pl.BlockSpec(memory_space=pltpu.VMEM)
HBM = pl.BlockSpec(memory_space=pltpu.HBM)


def far(x):
    return pltpu.with_memory_space_constraint(x, pltpu.HBM)


def f32(*shape):
    return jax.ShapeDtypeStruct(shape, jnp.float32)


def received(ref):
    return ref[...].reshape(ref.shape[0], ref.shape[2])


def send(out_ref, lanes, row):
    out_ref[:, :, lanes] = jnp.broadcast_to(row[None], (out_ref.shape[0], 1, row.shape[1]))


def combine(parts):
    top = jnp.max(parts, axis=0, keepdims=True)
    return top + jnp.log2(jnp.sum(jnp.exp2(parts - top), axis=0, keepdims=True))


def split(x):
    high = x.astype(jnp.bfloat16)
    low = (x - high.astype(jnp.float32)).astype(jnp.bfloat16)
    return high, low


def row_partials(score_ref, pot, out_ref, spread_ref):
    rows, width = score_ref.shape
    tiles = width // LANES
    pots = None if pot is None else jnp.broadcast_to(pot, (SUBS, width))

    def body(group, carry):
        base = pl.multiple_of(group * SUBS, SUBS)
        values = []
        for tile in range(tiles):
            value = score_ref[pl.ds(base, SUBS), tile * LANES : (tile + 1) * LANES]
            if pots is not None:
                value = value + pots[:, tile * LANES : (tile + 1) * LANES]
            values.append(value)
        top = values[0]
        for value in values[1:]:
            top = jnp.maximum(top, value)
        total = jnp.exp2(values[0] - top)
        for value in values[1:]:
            total = total + jnp.exp2(value - top)
        spread_ref[pl.ds(base, SUBS), :] = top + jnp.log2(total)
        return carry

    lax.fori_loop(0, rows // SUBS, body, 0, unroll=4)
    for block in range(rows // LANES):
        lanes = slice(block * LANES, (block + 1) * LANES)
        send(out_ref, lanes, combine(spread_ref[lanes, :].T))


def spread_rows(pot, spread_ref):
    for block in range(pot.shape[1] // LANES):
        part = pot[:, block * LANES : (block + 1) * LANES]
        spread_ref[block * LANES : (block + 1) * LANES, :] = jnp.broadcast_to(part, (LANES, LANES)).T


def col_stats(score_ref, spread_ref, tile, chunk=16):
    rows = score_ref.shape[0]
    lanes = slice(tile * LANES, (tile + 1) * LANES)

    def body(step, carry):
        old_top, old_total = carry
        values = []
        for index in range(chunk):
            base = pl.multiple_of(step * (chunk * SUBS), chunk * SUBS) + index * SUBS
            values.append(score_ref[pl.ds(base, SUBS), lanes] + spread_ref[pl.ds(base, SUBS), :])
        top = old_top
        for value in values:
            top = jnp.maximum(top, value)
        total = old_total * jnp.exp2(old_top - top)
        for value in values:
            total = total + jnp.exp2(value - top)
        return top, total

    start = (jnp.full((SUBS, LANES), -1e30, jnp.float32), jnp.zeros((SUBS, LANES), jnp.float32))
    return lax.fori_loop(0, rows // (chunk * SUBS), body, start, unroll=2)


def lane_sums(ref, out_ref, scale):
    for block in range(ref.shape[0] // LANES):
        part = ref[block * LANES : (block + 1) * LANES, :]
        out_ref[:, block * LANES : (block + 1) * LANES] = (
            jnp.sum((part * part).T, axis=0, keepdims=True) * scale
        )


def first_kernel(
    place_ref, particles_hbm, weights_hbm, targets_hbm,
    score_ref, out_ref, source_sq_ref, weights_ref, mine_ref, mine_sq_ref,
    particles_ref, targets_ref, right_ref, points_sq_ref, spread_ref, sems,
):
    size = particles_ref.shape[1]
    scale = LOG2E / (EPS * size)
    rows = particles_ref.shape[0]
    copies = [
        pltpu.make_async_copy(targets_hbm, targets_ref, sems.at[0]),
        pltpu.make_async_copy(particles_hbm, particles_ref, sems.at[1]),
        pltpu.make_async_copy(weights_hbm, weights_ref, sems.at[2]),
    ]
    for copy in copies:
        copy.start()
    copies[0].wait()
    high, low = split(targets_ref[...])
    right_ref[...] = jnp.concatenate([high, low, high, low], axis=1)
    lane_sums(targets_ref, points_sq_ref, scale)
    count = mine_ref.shape[0]
    mine = targets_ref[pl.ds(pl.multiple_of(place_ref[0] * count, SUBS), count), :]
    high, low = split(mine * (2.0 * scale))
    mine_ref[...] = jnp.concatenate([high, high, low, low], axis=1)
    mine_sq_ref[...] = jnp.broadcast_to(jnp.sum(mine * mine, axis=1, keepdims=True) * scale, mine_sq_ref.shape)
    copies[1].wait()
    lane_sums(particles_ref, source_sq_ref, scale)
    points_sq = points_sq_ref[...]
    step = 256

    def body(index, carry):
        base = pl.multiple_of(index * step, step)
        source = particles_ref[pl.ds(base, step), :]
        source_sq = jnp.sum(source * source, axis=1, keepdims=True) * scale
        high, low = split(source * (2.0 * scale))
        left = jnp.concatenate([high, high, low, low], axis=1)
        cross = lax.dot_general(
            left, right_ref[...], (((1,), (1,)), ((), ())), preferred_element_type=jnp.float32
        )
        score_ref[pl.ds(base, step), :] = cross - source_sq - points_sq
        return carry

    lax.fori_loop(0, rows // step, body, 0)
    row_partials(score_ref, None, out_ref, spread_ref)
    copies[2].wait()


def row_kernel(log_count, score_ref, parts_ref, out_ref, spread_ref):
    col_pot = -log_count - combine(received(parts_ref))
    row_partials(score_ref, col_pot, out_ref, spread_ref)


def col_kernel(score_ref, parts_ref, weights_ref, out_ref, spread_ref):
    row_pot = weights_ref[...] * LOG2E - combine(received(parts_ref))
    spread_rows(row_pot, spread_ref)
    for tile in range(score_ref.shape[1] // LANES):
        top, total = col_stats(score_ref, spread_ref, tile)
        send(out_ref, slice(tile * LANES, (tile + 1) * LANES), combine(top + jnp.log2(total)))


def pot_kernel(parts_ref, weights_ref, source_sq_ref, out_ref):
    pot = weights_ref[...] * LOG2E - combine(received(parts_ref)) - source_sq_ref[...]
    send(out_ref, slice(0, pot.shape[1]), pot)


def cross_kernel(particles_ref, mine_ref, mine_sq_ref, cross_ref, half_ref):
    blocks, _, rows = cross_ref.shape
    for block in range(blocks):
        high, low = split(particles_ref[block * rows : (block + 1) * rows, :])
        half_ref[block] = high
        right = jnp.concatenate([high, low, high, low], axis=1)
        cross = lax.dot_general(
            mine_ref[...], right, (((1,), (1,)), ((), ())), preferred_element_type=jnp.float32
        )
        cross_ref[block] = cross - mine_sq_ref[:, :1]


def last_kernel(cross_hbm, pots_ref, half_hbm, out_ref, cross_ref, half_ref, plan_ref, sems):
    blocks, width, rows = cross_ref.shape
    tiles = rows // LANES

    def copy(which, block):
        source, target = ((cross_hbm, cross_ref), (half_hbm, half_ref))[which]
        return pltpu.make_async_copy(source.at[block], target.at[block], sems.at[which, block])

    for which in range(2):
        for block in range(blocks):
            copy(which, block).start()

    def largest(block, tops):
        copy(0, block).wait()
        pots = jnp.broadcast_to(pots_ref[block], (SUBS, rows))
        news = []
        for group in range(width // SUBS):
            top = tops[group]
            for tile in range(tiles):
                lanes = slice(tile * LANES, (tile + 1) * LANES)
                top = jnp.maximum(top, cross_ref[block, group * SUBS : (group + 1) * SUBS, lanes] + pots[:, lanes])
            news.append(top)
        return tuple(news)

    start = tuple(jnp.full((SUBS, LANES), -1e30, jnp.float32) for _ in range(width // SUBS))
    tops = lax.fori_loop(0, blocks, largest, start)
    tops = [jnp.broadcast_to(jnp.max(top, axis=1, keepdims=True), (SUBS, LANES)) for top in tops]

    def fill(block, carry):
        totals, acc = carry
        pots = jnp.broadcast_to(pots_ref[block], (SUBS, rows))
        news = []
        for group in range(0, width // SUBS, 2):
            pair = []
            for index in (group, group + 1):
                values = []
                total = totals[index]
                for tile in range(tiles):
                    lanes = slice(tile * LANES, (tile + 1) * LANES)
                    value = jnp.exp2(
                        cross_ref[block, index * SUBS : (index + 1) * SUBS, lanes] + pots[:, lanes] - tops[index]
                    )
                    values.append(value)
                    total = total + value
                news.append(total)
                pair.append(values)
            for tile in range(tiles):
                plan_ref[group * SUBS : (group + 2) * SUBS, tile * LANES : (tile + 1) * LANES] = jnp.concatenate(
                    [pair[0][tile], pair[1][tile]], axis=0
                ).astype(jnp.bfloat16)
        copy(1, block).wait()
        acc = acc + jnp.dot(plan_ref[...], half_ref[block], preferred_element_type=jnp.float32)
        return tuple(news), acc

    zeros = tuple(jnp.zeros((SUBS, LANES), jnp.float32) for _ in range(width // SUBS))
    totals, acc = lax.fori_loop(0, blocks, fill, (zeros, jnp.zeros(out_ref.shape, jnp.float32)))
    total = jnp.concatenate([jnp.sum(total, axis=1, keepdims=True) for total in totals], axis=0)
    out_ref[...] = acc / total


def exchange(sent, axis):
    return lax.all_to_all(sent, axis, 0, 0, tiled=True)


def per_device(particles, log_weights, targets):
    rows, size = particles.shape
    width = targets.shape[0]
    row_axes, col_axes = ("y", "core"), ("z", "x")
    row_count = lax.axis_size(row_axes)
    log_count = math.log2(width * lax.axis_size(col_axes))
    params = pltpu.CompilerParams(vmem_limit_bytes=12 * 1024 * 1024)
    spread = pltpu.VMEM((rows, LANES), jnp.float32)
    kept = pltpu.VMEM((rows, width), jnp.float32)
    block = width // row_count
    place = lax.axis_index(row_axes).astype(jnp.int32).reshape(1)
    every = lax.all_gather(particles, row_axes, tiled=True)
    to_cols = f32(lax.axis_size(col_axes), 1, rows)
    to_rows = f32(row_count, 1, width)

    score, local, source_sq, weights, mine, mine_sq = pl.pallas_call(
        first_kernel,
        out_shape=(
            kept, to_cols, f32(1, rows), f32(1, rows),
            jax.ShapeDtypeStruct((block, 4 * size), jnp.bfloat16), f32(block, LANES),
        ),
        in_specs=[pl.BlockSpec(memory_space=pltpu.SMEM)] + [HBM] * 3,
        out_specs=(VMEM,) * 6,
        scratch_shapes=[
            pltpu.VMEM((rows, size), jnp.float32),
            pltpu.VMEM((width, size), jnp.float32),
            pltpu.VMEM((width, 4 * size), jnp.bfloat16),
            pltpu.VMEM((1, width), jnp.float32),
            spread,
            pltpu.SemaphoreType.DMA((3,)),
        ],
        compiler_params=params,
    )(place, far(particles), far(log_weights.reshape(1, rows)), far(targets))
    for iteration in range(ITERS):
        if iteration:
            local = pl.pallas_call(
                lambda *refs: row_kernel(log_count, *refs),
                name="row_kernel",
                out_shape=to_cols,
                in_specs=[VMEM] * 2,
                out_specs=VMEM,
                scratch_shapes=[spread],
                compiler_params=params,
            )(score, parts)
        if iteration == ITERS - 1:
            local, every = lax.optimization_barrier((local, every))
        parts = exchange(local, col_axes)
        if iteration == ITERS - 1:
            break
        local = pl.pallas_call(
            col_kernel,
            out_shape=to_rows,
            in_specs=[VMEM] * 3,
            out_specs=VMEM,
            scratch_shapes=[spread],
            compiler_params=params,
        )(score, parts, weights)
        parts = exchange(local, row_axes)
    step = 2
    cross, half = pl.pallas_call(
        cross_kernel,
        grid=(row_count // step,),
        out_shape=(
            pltpu.HBM((row_count, block, rows), jnp.float32),
            pltpu.HBM((row_count, rows, size), jnp.bfloat16),
        ),
        in_specs=[
            pl.BlockSpec((step * rows, size), lambda index: (index, 0)),
            pl.BlockSpec((block, 4 * size), lambda index: (0, 0)),
            pl.BlockSpec((block, LANES), lambda index: (0, 0)),
        ],
        out_specs=(
            pl.BlockSpec((step, block, rows), lambda index: (index, 0, 0)),
            pl.BlockSpec((step, rows, size), lambda index: (index, 0, 0)),
        ),
        compiler_params=pltpu.CompilerParams(vmem_limit_bytes=16 * 1024 * 1024),
        cost_estimate=pl.CostEstimate(
            flops=8 * row_count * rows * block * size,
            bytes_accessed=row_count * rows * (6 * size + 4 * block),
            transcendentals=0,
        ),
    )(far(every), mine, mine_sq)
    parts, cross, half = lax.optimization_barrier((parts, cross, half))
    pots = pl.pallas_call(
        pot_kernel,
        out_shape=f32(row_count, 1, rows),
        in_specs=[VMEM] * 3,
        out_specs=VMEM,
        compiler_params=params,
    )(parts, weights, source_sq)
    pots = exchange(pots, row_axes)
    return pl.pallas_call(
        last_kernel,
        out_shape=f32(block, size),
        in_specs=[HBM, VMEM, HBM],
        out_specs=VMEM,
        scratch_shapes=[
            pltpu.VMEM((row_count, block, rows), jnp.float32),
            pltpu.VMEM((row_count, rows, size), jnp.bfloat16),
            pltpu.VMEM((block, rows), jnp.bfloat16),
            pltpu.SemaphoreType.DMA((2, row_count)),
        ],
        compiler_params=pltpu.CompilerParams(vmem_limit_bytes=16 * 1024 * 1024),
    )(far(cross), pots, far(half))


def solution(mesh):
    shape = dict(mesh.shape)
    row, col = shape["row"], shape["col"]
    devices = mesh.devices.reshape(row // 2, 2, col // 4, 4)
    parts = jax.sharding.Mesh(devices, ("y", "core", "z", "x"))
    rows, cols = ("y", "core"), ("z", "x")
    return jax.shard_map(
        per_device,
        mesh=parts,
        in_specs=(P(rows, None), P(rows), P(cols, None)),
        out_specs=P(cols + rows, None),
        check_vma=False,
    )
```

```python
import math

import jax
import jax.numpy as jnp
from jax import lax
from jax.experimental import pallas as pl
from jax.experimental.pallas import tpu as pltpu
from jax.sharding import PartitionSpec as P

ITERS = 3
EPS = 0.01
LOG2E = math.log2(math.e)
LANES = 128
SUBS = 8
CHUNK = 128
STATS = 8
LOWEST = -1e30
VMEM = pl.BlockSpec(memory_space=pltpu.VMEM)
HBM = pl.BlockSpec(memory_space=pltpu.HBM)


def far(x):
    return pltpu.with_memory_space_constraint(x, pltpu.HBM)


def f32(*shape):
    return jax.ShapeDtypeStruct(shape, jnp.float32)


def lanes_of(tile):
    return slice(tile * LANES, (tile + 1) * LANES)


def received(ref):
    return ref[...].reshape(ref.shape[0], ref.shape[2])


def send(out_ref, lanes, row):
    out_ref[:, :, lanes] = jnp.broadcast_to(row[None], (out_ref.shape[0], 1, row.shape[1]))


def combine(parts):
    top = jnp.max(parts, axis=0, keepdims=True)
    return top + jnp.log2(jnp.sum(jnp.exp2(parts - top), axis=0, keepdims=True))


def split(x):
    high = x.astype(jnp.bfloat16)
    low = (x - high.astype(jnp.float32)).astype(jnp.bfloat16)
    return high, low


def tree(op, values):
    while len(values) > 1:
        values = [op(*values[i : i + 2]) if i + 1 < len(values) else values[i] for i in range(0, len(values), 2)]
    return values[0]


def lane_lse(values):
    top = tree(jnp.maximum, values)
    return top + jnp.log2(tree(jnp.add, [jnp.exp2(value - top) for value in values]))


def row_group(score_ref, base, pots, spread_ref):
    values = []
    for tile in range(score_ref.shape[1] // LANES):
        value = score_ref[pl.ds(base, SUBS), lanes_of(tile)]
        values.append(value if pots is None else value + pots[:, lanes_of(tile)])
    spread_ref[pl.ds(base, SUBS), :] = lane_lse(values)


def send_rows(spread_ref, out_ref):
    for block in range(spread_ref.shape[0] // LANES):
        send(out_ref, lanes_of(block), combine(spread_ref[lanes_of(block), :].T))


def spread_rows(pot, spread_ref):
    for block in range(pot.shape[1] // LANES):
        spread_ref[lanes_of(block), :] = jnp.broadcast_to(pot[:, lanes_of(block)], (LANES, LANES)).T


def first_kernel(
    particles_hbm, weights_hbm, targets_hbm,
    score_ref, out_ref, weights_ref, half_ref,
    particles_ref, targets_ref, right_ref, points_sq_ref, spread_ref, sems,
):
    rows, size = particles_ref.shape
    scale = LOG2E / (EPS * size)
    copies = [
        pltpu.make_async_copy(targets_hbm, targets_ref, sems.at[0]),
        pltpu.make_async_copy(particles_hbm, particles_ref, sems.at[1]),
        pltpu.make_async_copy(weights_hbm, weights_ref, sems.at[2]),
    ]
    for copy in copies:
        copy.start()
    copies[0].wait()
    for tile in range(targets_ref.shape[0] // LANES):
        lanes = lanes_of(tile)
        part = targets_ref[lanes, :].T
        points_sq_ref[:, lanes] = jnp.sum(part * part, axis=0, keepdims=True) * scale
        high, low = split(part)
        for index, half in enumerate((high, low, high, low)):
            right_ref[index * size : (index + 1) * size, lanes] = half
    copies[1].wait()
    copies[2].wait()
    points_sq = points_sq_ref[...]
    step = 256

    def scores(index):
        part = slice(index * step, (index + 1) * step)
        source = particles_ref[part, :]
        source_sq = jnp.sum(source * source, axis=1, keepdims=True) * scale
        high, low = split(source * (2.0 * scale))
        left = jnp.concatenate([high, high, low, low], axis=1)
        cross = jnp.dot(left, right_ref[...], preferred_element_type=jnp.float32)
        score_ref[part, :] = cross - source_sq - points_sq
        half_ref[:, part] = source.T.astype(jnp.bfloat16)

    def partials(index):
        for group in range(step // SUBS):
            row_group(score_ref, index * step + group * SUBS, None, spread_ref)

    for index in range(rows // step):
        scores(index)
        if index:
            partials(index - 1)
    partials(rows // step - 1)
    send_rows(spread_ref, out_ref)


def row_kernel(log_count, score_ref, parts_ref, out_ref, spread_ref):
    col_pot = -log_count - combine(received(parts_ref))
    pots = jnp.broadcast_to(col_pot, (SUBS, col_pot.shape[1]))

    def body(group, carry):
        row_group(score_ref, pl.multiple_of(group * SUBS, SUBS), pots, spread_ref)
        return carry

    lax.fori_loop(0, score_ref.shape[0] // SUBS, body, 0, unroll=8)
    send_rows(spread_ref, out_ref)


def col_chunk(score_ref, spread_ref, step):
    base = pl.multiple_of(step * CHUNK, CHUNK)
    pots = [spread_ref[pl.ds(base + index * SUBS, SUBS), :] for index in range(CHUNK // SUBS)]
    for tile in range(score_ref.shape[1] // LANES):
        yield tile, [
            score_ref[pl.ds(base + index * SUBS, SUBS), lanes_of(tile)] + pot for index, pot in enumerate(pots)
        ]


def col_kernel(score_ref, parts_ref, weights_ref, out_ref, spread_ref, chunk_ref):
    rows, width = score_ref.shape
    row_pot = weights_ref[...] * LOG2E - combine(received(parts_ref))
    spread_rows(row_pot, spread_ref)

    def body(step, carry):
        for tile, values in col_chunk(score_ref, spread_ref, step):
            chunk_ref[pl.ds(pl.multiple_of(step * SUBS, SUBS), SUBS), lanes_of(tile)] = lane_lse(values)
        return carry

    lax.fori_loop(0, rows // CHUNK, body, 0)
    send(out_ref, slice(0, width), combine(chunk_ref[...]))


def last_kernel(score_ref, parts_ref, weights_ref, half_ref, out_ref, spread_ref, plan_ref):
    rows, width = score_ref.shape
    tiles = width // LANES
    row_pot = weights_ref[...] * LOG2E - combine(received(parts_ref))
    spread_rows(row_pot, spread_ref)

    def largest(step, tops):
        news = []
        for tile, values in col_chunk(score_ref, spread_ref, step):
            news.append(jnp.maximum(tops[tile], tree(jnp.maximum, values)))
        return tuple(news)

    tops = lax.fori_loop(
        0, rows // CHUNK, largest, tuple(jnp.full((SUBS, LANES), LOWEST, jnp.float32) for _ in range(tiles))
    )
    top = jnp.concatenate([jnp.max(top, axis=0, keepdims=True) for top in tops], axis=1)
    every = jnp.broadcast_to(top, (SUBS, width))

    def fill(step, totals):
        news = []
        for tile, values in col_chunk(score_ref, spread_ref, step):
            values = [jnp.exp2(value - every[:, lanes_of(tile)]) for value in values]
            news.append(totals[tile] + tree(jnp.add, values))
            for index in range(0, len(values), 2):
                base = pl.multiple_of(step * CHUNK, CHUNK) + index * SUBS
                plan_ref[pl.ds(base, 2 * SUBS), lanes_of(tile)] = jnp.concatenate(
                    values[index : index + 2], axis=0
                ).astype(jnp.bfloat16)
        return tuple(news)

    totals = lax.fori_loop(
        0, rows // CHUNK, fill, tuple(jnp.zeros((SUBS, LANES), jnp.float32) for _ in range(tiles))
    )
    total = jnp.concatenate([jnp.sum(total, axis=0, keepdims=True) for total in totals], axis=1)
    sums = jnp.dot(half_ref[...], plan_ref[...], preferred_element_type=jnp.float32)
    sums = jnp.concatenate([sums[:, lanes_of(tile)].T for tile in range(tiles)], axis=0)
    cores, chips, block = out_ref.shape[0], out_ref.shape[1], out_ref.shape[2] - STATS
    rest = jnp.zeros((1, LANES - block), jnp.float32)
    for chip in range(chips):
        for core in range(cores):
            start = (chip * cores + core) * block
            out_ref[core, chip, :block, :] = sums[start : start + block]
            for index, row in enumerate((top, total)):
                out_ref[core, chip, block + index : block + index + 1, :] = jnp.concatenate(
                    [row[:, start : start + block], rest], axis=1
                )
            out_ref[core, chip, block + 2 :, :] = jnp.zeros((STATS - 2, LANES), jnp.float32)


def exchange(sent, axis):
    return lax.all_to_all(sent, axis, 0, 0, tiled=True)


def merge(blocks, block):
    sums = blocks[..., :block, :]
    tops = blocks[..., block, :block]
    totals = blocks[..., block + 1, :block]
    top = jnp.max(tops, axis=0)
    weight = jnp.exp2(tops - top[None])
    return jnp.sum(sums * weight[..., None], axis=0), top, jnp.sum(totals * weight, axis=0)


def pack(sums, tops, totals):
    stats = jnp.stack([tops, totals], axis=-2)
    pad = [(0, STATS - 2), (0, LANES - tops.shape[-1])]
    stats = jnp.pad(stats, [(0, 0)] * (stats.ndim - 2) + pad)
    return jnp.concatenate([sums, stats], axis=-2)


def per_device(particles, log_weights, targets):
    rows, size = particles.shape
    width = targets.shape[0]
    row_axes, col_axes = ("y", "core"), ("z", "x")
    chips, cores = lax.axis_size("y"), lax.axis_size("core")
    block = width // (chips * cores)
    log_count = math.log2(width * lax.axis_size(col_axes))
    params = pltpu.CompilerParams(vmem_limit_bytes=12 * 1024 * 1024)
    spread = pltpu.VMEM((rows, LANES), jnp.float32)
    to_cols = f32(lax.axis_size(col_axes), 1, rows)
    to_rows = f32(chips * cores, 1, width)

    score, local, weights, half = pl.pallas_call(
        first_kernel,
        out_shape=(f32(rows, width), to_cols, f32(1, rows), jax.ShapeDtypeStruct((size, rows), jnp.bfloat16)),
        in_specs=[HBM] * 3,
        out_specs=(VMEM,) * 4,
        scratch_shapes=[
            pltpu.VMEM((rows, size), jnp.float32),
            pltpu.VMEM((width, size), jnp.float32),
            pltpu.VMEM((4 * size, width), jnp.bfloat16),
            pltpu.VMEM((1, width), jnp.float32),
            spread,
            pltpu.SemaphoreType.DMA((3,)),
        ],
        compiler_params=params,
    )(far(particles), far(log_weights.reshape(1, rows)), far(targets))
    for iteration in range(ITERS):
        if iteration:
            local = pl.pallas_call(
                lambda *refs: row_kernel(log_count, *refs),
                name="row_kernel",
                out_shape=to_cols,
                in_specs=[VMEM] * 2,
                out_specs=VMEM,
                scratch_shapes=[spread],
                compiler_params=params,
            )(score, parts)
        parts = exchange(local, col_axes)
        if iteration == ITERS - 1:
            break
        local = pl.pallas_call(
            col_kernel,
            out_shape=to_rows,
            in_specs=[VMEM] * 3,
            out_specs=VMEM,
            scratch_shapes=[spread, pltpu.VMEM((rows // CHUNK * SUBS, width), jnp.float32)],
            compiler_params=params,
        )(score, parts, weights)
        parts = exchange(local, row_axes)
    blocks = pl.pallas_call(
        last_kernel,
        out_shape=f32(cores, chips, block + STATS, size),
        in_specs=[VMEM] * 4,
        out_specs=VMEM,
        scratch_shapes=[spread, pltpu.VMEM((rows, width), jnp.bfloat16)],
        compiler_params=params,
    )(score, parts, weights, half)
    blocks = exchange(blocks, "core")
    blocks = exchange(pack(*merge(blocks, block)), "y")
    sums, _, total = merge(blocks, block)
    return sums / total[:, None]


def solution(mesh):
    shape = dict(mesh.shape)
    row, col = shape["row"], shape["col"]
    devices = mesh.devices.reshape(row // 2, 2, col // 4, 4)
    parts = jax.sharding.Mesh(devices, ("y", "core", "z", "x"))
    rows, cols = ("y", "core"), ("z", "x")
    return jax.shard_map(
        per_device,
        mesh=parts,
        in_specs=(P(rows, None), P(rows), P(cols, None)),
        out_specs=P(cols + rows, None),
        check_vma=False,
    )
```

```python
import math

import jax
import jax.numpy as jnp
from jax import lax
from jax.experimental import pallas as pl
from jax.experimental.pallas import tpu as pltpu
from jax.sharding import PartitionSpec as P

ITERS = 3
EPS = 0.01
LOG2E = math.log2(math.e)
LANES = 128
SUBS = 8
CHUNK = 128
STATS = 8
LOWEST = -1e30
VMEM = pl.BlockSpec(memory_space=pltpu.VMEM)
HBM = pl.BlockSpec(memory_space=pltpu.HBM)


def far(x):
    return pltpu.with_memory_space_constraint(x, pltpu.HBM)


def f32(*shape):
    return jax.ShapeDtypeStruct(shape, jnp.float32)


def lanes_of(tile):
    return slice(tile * LANES, (tile + 1) * LANES)


def received(ref):
    return ref[...].reshape(ref.shape[0], ref.shape[2])


def send(out_ref, lanes, row):
    out_ref[:, :, lanes] = jnp.broadcast_to(row[None], (out_ref.shape[0], 1, row.shape[1]))


def combine(parts):
    top = jnp.max(parts, axis=0, keepdims=True)
    return top + jnp.log2(jnp.sum(jnp.exp2(parts - top), axis=0, keepdims=True))


def split(x):
    high = x.astype(jnp.bfloat16)
    low = (x - high.astype(jnp.float32)).astype(jnp.bfloat16)
    return high, low


def tree(op, values):
    while len(values) > 1:
        values = [op(*values[i : i + 2]) if i + 1 < len(values) else values[i] for i in range(0, len(values), 2)]
    return values[0]


def lane_lse(values):
    top = tree(jnp.maximum, values)
    return top + jnp.log2(tree(jnp.add, [jnp.exp2(value - top) for value in values]))


def row_group(score_ref, base, pots, spread_ref):
    values = []
    tiles = score_ref.shape[2] // LANES
    for tile in range(score_ref.shape[0] * tiles):
        value = score_ref[tile // tiles, pl.ds(base, SUBS), lanes_of(tile % tiles)]
        values.append(value if pots is None else value + pots[:, lanes_of(tile)])
    spread_ref[pl.ds(base, SUBS), :] = lane_lse(values)


def send_rows(spread_ref, out_ref):
    for block in range(spread_ref.shape[0] // LANES):
        send(out_ref, lanes_of(block), combine(spread_ref[lanes_of(block), :].T))


def spread_rows(pot, spread_ref):
    for block in range(pot.shape[1] // LANES):
        spread_ref[lanes_of(block), :] = jnp.broadcast_to(pot[:, lanes_of(block)], (LANES, LANES)).T


def first_kernel(
    chips, cores, particles_hbm, weights_hbm, targets_hbm,
    score_ref, out_ref, weights_ref, half_ref,
    particles_ref, targets_ref, right_ref, points_sq_ref, spread_ref, sems,
):
    rows, size = particles_ref.shape
    width = targets_ref.shape[0]
    block = width // (chips * cores)
    scale = LOG2E / (EPS * size)
    copies = [
        pltpu.make_async_copy(targets_hbm, targets_ref, sems.at[0]),
        pltpu.make_async_copy(particles_hbm, particles_ref, sems.at[1]),
        pltpu.make_async_copy(weights_hbm, weights_ref, sems.at[2]),
    ]
    for copy in copies:
        copy.start()
    copies[0].wait()
    for tile in range(width // LANES):
        lanes = lanes_of(tile)
        parts, place = [], lanes.start
        while place < lanes.stop:
            core, chip = divmod(place // block, chips)
            count = min(lanes.stop, (place // block + 1) * block) - place
            start = (chip * cores + core) * block + place % block
            parts.append(targets_ref[start : start + count, :])
            place += count
        part = jnp.concatenate(parts, axis=0).T
        points_sq_ref[:, lanes] = jnp.sum(part * part, axis=0, keepdims=True) * scale
        high, low = split(part)
        for index, half in enumerate((high, low, high, low)):
            right_ref[index * size : (index + 1) * size, lanes] = half
    copies[1].wait()
    copies[2].wait()
    points_sq = points_sq_ref[...]
    step = 256

    def scores(index):
        part = slice(index * step, (index + 1) * step)
        source = particles_ref[part, :]
        source_sq = jnp.sum(source * source, axis=1, keepdims=True) * scale
        high, low = split(source * (2.0 * scale))
        left = jnp.concatenate([high, high, low, low], axis=1)
        cross = jnp.dot(left, right_ref[...], preferred_element_type=jnp.float32)
        cross = cross - source_sq - points_sq
        for core in range(cores):
            score_ref[core, part, :] = cross[:, core * width // cores : (core + 1) * width // cores]
        half_ref[:, part] = source.T.astype(jnp.bfloat16)

    def partials(index):
        for group in range(step // SUBS):
            row_group(score_ref, index * step + group * SUBS, None, spread_ref)

    for index in range(rows // step):
        scores(index)
        if index:
            partials(index - 1)
    partials(rows // step - 1)
    send_rows(spread_ref, out_ref)


def row_kernel(log_count, score_ref, parts_ref, out_ref, spread_ref):
    col_pot = -log_count - combine(received(parts_ref))
    pots = jnp.broadcast_to(col_pot, (SUBS, col_pot.shape[1]))

    def body(group, carry):
        row_group(score_ref, pl.multiple_of(group * SUBS, SUBS), pots, spread_ref)
        return carry

    lax.fori_loop(0, score_ref.shape[1] // SUBS, body, 0, unroll=16)
    send_rows(spread_ref, out_ref)


def col_chunk(score_ref, spread_ref, step):
    base = step * CHUNK if isinstance(step, int) else pl.multiple_of(step * CHUNK, CHUNK)
    pots = [spread_ref[pl.ds(base + index * SUBS, SUBS), :] for index in range(CHUNK // SUBS)]
    for tile in range(score_ref.shape[1] // LANES):
        yield tile, [
            score_ref[pl.ds(base + index * SUBS, SUBS), lanes_of(tile)] + pot for index, pot in enumerate(pots)
        ]


def col_kernel(score_ref, parts_ref, weights_ref, out_ref, spread_ref, chunk_ref):
    cores, rows, width = score_ref.shape
    row_pot = weights_ref[...] * LOG2E - combine(received(parts_ref))
    spread_rows(row_pot, spread_ref)

    def body(step, carry):
        for core in range(cores):
            for tile, values in col_chunk(score_ref.at[core], spread_ref, step):
                lanes = lanes_of(core * width // LANES + tile)
                chunk_ref[pl.ds(pl.multiple_of(step * SUBS, SUBS), SUBS), lanes] = lane_lse(values)
        return carry

    lax.fori_loop(0, rows // CHUNK, body, 0)
    send(out_ref, slice(0, cores * width), combine(chunk_ref[...]))


def half_sums(score_ref, half_ref, spread_ref, out_ref, plan_ref):
    rows, width = score_ref.shape
    size = half_ref.shape[0]
    tiles = width // LANES

    def largest(step, tops):
        news = []
        for tile, values in col_chunk(score_ref, spread_ref, step):
            news.append(jnp.maximum(tops[tile], tree(jnp.maximum, values)))
        return tuple(news)

    tops = lax.fori_loop(
        0, rows // CHUNK, largest, tuple(jnp.full((SUBS, LANES), LOWEST, jnp.float32) for _ in range(tiles))
    )
    top = jnp.concatenate([jnp.max(top, axis=0, keepdims=True) for top in tops], axis=1)
    every = jnp.broadcast_to(top, (SUBS, width))
    totals = [jnp.zeros((SUBS, LANES), jnp.float32) for _ in range(tiles)]
    depth = 2 * CHUNK
    for part in range(rows // depth):
        for step in range(part * depth // CHUNK, (part + 1) * depth // CHUNK):
            for tile, values in col_chunk(score_ref, spread_ref, step):
                values = [jnp.exp2(value - every[:, lanes_of(tile)]) for value in values]
                totals[tile] = totals[tile] + tree(jnp.add, values)
                for index in range(0, len(values), 2):
                    base = step * CHUNK + index * SUBS
                    plan_ref[base : base + 2 * SUBS, lanes_of(tile)] = jnp.concatenate(
                        values[index : index + 2], axis=0
                    ).astype(jnp.bfloat16)
        inner = slice(part * depth, (part + 1) * depth)
        sums = jnp.dot(half_ref[:, inner], plan_ref[inner, :], preferred_element_type=jnp.float32)
        out_ref[:size, :] = out_ref[:size, :] + sums if part else sums
    total = jnp.concatenate([jnp.sum(total, axis=0, keepdims=True) for total in totals], axis=1)
    out_ref[size:, :] = jnp.concatenate([top, total, jnp.zeros((STATS - 2, width), jnp.float32)], axis=0)


def sibling_kernel(score_ref, parts_ref, weights_ref, half_ref, out_ref, spread_ref, plan_ref):
    row_pot = weights_ref[...] * LOG2E - combine(received(parts_ref))
    spread_rows(row_pot, spread_ref)
    half_sums(score_ref.at[1 - lax.axis_index("core")], half_ref, spread_ref, out_ref, plan_ref)


def own_kernel(score_ref, spread_ref, half_ref, out_ref, plan_ref):
    half_sums(score_ref.at[lax.axis_index("core")], half_ref, spread_ref, out_ref, plan_ref)


def join_kernel(own_ref, other_ref, out_ref):
    chips, block = out_ref.shape[0], out_ref.shape[1] - STATS
    size = own_ref.shape[0] - STATS
    tops = [ref[size : size + 1, :] for ref in (own_ref, other_ref)]
    top = jnp.maximum(*tops)
    own, other = (jnp.exp2(value - top) for value in tops)
    total = own_ref[size + 1 : size + 2, :] * own + other_ref[size + 1 : size + 2, :] * other
    sums = []
    for tile in range(own_ref.shape[1] // LANES):
        lanes = lanes_of(tile)
        sums.append((own_ref[:size, lanes] * own[:, lanes] + other_ref[:size, lanes] * other[:, lanes]).T)
    sums = jnp.concatenate(sums, axis=0)
    rest = jnp.zeros((1, LANES - block), jnp.float32)
    for chip in range(chips):
        part = slice(chip * block, (chip + 1) * block)
        out_ref[chip, :block, :] = sums[part]
        stats = [jnp.concatenate([row[:, part], rest], axis=1) for row in (top, total)]
        out_ref[chip, block:, :] = jnp.concatenate(stats + [jnp.zeros((STATS - 2, LANES), jnp.float32)], axis=0)


def final_kernel(blocks_ref, out_ref):
    chips, block = blocks_ref.shape[0], out_ref.shape[0]
    tops = [blocks_ref[chip, block : block + 1, :] for chip in range(chips)]
    top = tree(jnp.maximum, tops)
    shares = [jnp.exp2(value - top) for value in tops]
    total = tree(jnp.add, [blocks_ref[chip, block + 1 : block + 2, :] * share for chip, share in enumerate(shares)])
    scale = 1.0 / jnp.where(total > 0.0, total, 1.0)
    shares = jnp.concatenate([share * scale for share in shares], axis=0)
    shares = jnp.concatenate([shares, jnp.zeros((LANES - chips, LANES), jnp.float32)], axis=0).T
    out_ref[...] = tree(
        jnp.add, [blocks_ref[chip, :block, :] * shares[:block, chip : chip + 1] for chip in range(chips)]
    )


def exchange(sent, axis):
    return lax.all_to_all(sent, axis, 0, 0, tiled=True)


def per_device(particles, log_weights, targets):
    rows, size = particles.shape
    width = targets.shape[0]
    row_axes, col_axes = ("y", "core"), ("z", "x")
    chips, cores = lax.axis_size("y"), lax.axis_size("core")
    block = width // (chips * cores)
    log_count = math.log2(width * lax.axis_size(col_axes))
    params = pltpu.CompilerParams(vmem_limit_bytes=12 * 1024 * 1024)
    spread = pltpu.VMEM((rows, LANES), jnp.float32)
    to_cols = f32(lax.axis_size(col_axes), 1, rows)
    to_rows = f32(chips * cores, 1, width)

    score, local, weights, half = pl.pallas_call(
        lambda *refs: first_kernel(chips, cores, *refs),
        name="first_kernel",
        out_shape=(f32(cores, rows, width // cores), to_cols, f32(1, rows), jax.ShapeDtypeStruct((size, rows), jnp.bfloat16)),
        in_specs=[HBM] * 3,
        out_specs=(VMEM,) * 4,
        scratch_shapes=[
            pltpu.VMEM((rows, size), jnp.float32),
            pltpu.VMEM((width, size), jnp.float32),
            pltpu.VMEM((4 * size, width), jnp.bfloat16),
            pltpu.VMEM((1, width), jnp.float32),
            spread,
            pltpu.SemaphoreType.DMA((3,)),
        ],
        compiler_params=params,
    )(far(particles), far(log_weights.reshape(1, rows)), far(targets))
    for iteration in range(ITERS):
        if iteration:
            local = pl.pallas_call(
                lambda *refs: row_kernel(log_count, *refs),
                name="row_kernel",
                out_shape=to_cols,
                in_specs=[VMEM] * 2,
                out_specs=VMEM,
                scratch_shapes=[spread],
                compiler_params=params,
            )(score, parts)
        parts = exchange(local, col_axes)
        if iteration == ITERS - 1:
            break
        local = pl.pallas_call(
            col_kernel,
            out_shape=to_rows,
            in_specs=[VMEM] * 3,
            out_specs=VMEM,
            scratch_shapes=[spread, pltpu.VMEM((rows // CHUNK * SUBS, width), jnp.float32)],
            compiler_params=params,
        )(score, parts, weights)
        parts = exchange(local, row_axes)
    part = f32(size + STATS, width // cores)
    plan = pltpu.VMEM((rows, width // cores), jnp.bfloat16)
    sent, spreads = pl.pallas_call(
        sibling_kernel,
        out_shape=(part, f32(rows, LANES)),
        in_specs=[VMEM] * 4,
        out_specs=(VMEM,) * 2,
        scratch_shapes=[plan],
        compiler_params=params,
    )(score, parts, weights, half)
    other = lax.ppermute(sent, "core", [(core, (core + 1) % cores) for core in range(cores)])
    own = pl.pallas_call(
        own_kernel,
        out_shape=part,
        in_specs=[VMEM] * 3,
        out_specs=VMEM,
        scratch_shapes=[plan],
        compiler_params=params,
        cost_estimate=pl.CostEstimate(
            flops=2 * rows * width * size // cores,
            bytes_accessed=4 * rows * width // cores,
            transcendentals=rows * width // cores,
        ),
    )(score, spreads, half)
    blocks = pl.pallas_call(
        join_kernel,
        out_shape=f32(chips, block + STATS, size),
        in_specs=[VMEM] * 2,
        out_specs=VMEM,
        compiler_params=params,
    )(own, other)
    blocks = exchange(blocks, "y")
    return pl.pallas_call(
        final_kernel,
        out_shape=f32(block, size),
        in_specs=[VMEM],
        out_specs=VMEM,
        compiler_params=params,
    )(blocks)


def solution(mesh):
    shape = dict(mesh.shape)
    row, col = shape["row"], shape["col"]
    devices = mesh.devices.reshape(row // 2, 2, col // 4, 4)
    parts = jax.sharding.Mesh(devices, ("y", "core", "z", "x"))
    rows, cols = ("y", "core"), ("z", "x")
    return jax.shard_map(
        per_device,
        mesh=parts,
        in_specs=(P(rows, None), P(rows), P(cols, None)),
        out_specs=P(cols + rows, None),
        check_vma=False,
    )
```

```python
import math

import jax
import jax.numpy as jnp
from jax import lax
from jax.experimental import pallas as pl
from jax.experimental.pallas import tpu as pltpu
from jax.sharding import PartitionSpec as P

ITERS = 3
EPS = 0.01
LOG2E = math.log2(math.e)
LANES = 128
SUBS = 8
CHUNK = 128
STATS = 8
LOWEST = -1e30
VMEM = pl.BlockSpec(memory_space=pltpu.VMEM)
HBM = pl.BlockSpec(memory_space=pltpu.HBM)


def far(x):
    return pltpu.with_memory_space_constraint(x, pltpu.HBM)


def f32(*shape):
    return jax.ShapeDtypeStruct(shape, jnp.float32)


def lanes_of(tile):
    return slice(tile * LANES, (tile + 1) * LANES)


def received(ref):
    return ref[...].reshape(ref.shape[0], ref.shape[2])


def send(out_ref, lanes, row):
    out_ref[:, :, lanes] = jnp.broadcast_to(row[None], (out_ref.shape[0], 1, row.shape[1]))


def combine(parts):
    top = jnp.max(parts, axis=0, keepdims=True)
    return top + jnp.log2(jnp.sum(jnp.exp2(parts - top), axis=0, keepdims=True))


def split(x):
    high = x.astype(jnp.bfloat16)
    low = (x - high.astype(jnp.float32)).astype(jnp.bfloat16)
    return high, low


def tree(op, values):
    while len(values) > 1:
        values = [op(*values[i : i + 2]) if i + 1 < len(values) else values[i] for i in range(0, len(values), 2)]
    return values[0]


def lane_lse(values):
    top = tree(jnp.maximum, values)
    return top + jnp.log2(tree(jnp.add, [jnp.exp2(value - top) for value in values]))


def row_group(score_ref, base, pots, spread_ref):
    rows = slice(base, base + SUBS)
    values = []
    for core in range(score_ref.shape[0]):
        for tile in range(score_ref.shape[2] // LANES):
            value = score_ref[core, rows, lanes_of(tile)]
            values.append(value if pots is None else value + pots[core][:, lanes_of(tile)])
    spread_ref[rows, :] = lane_lse(values)


def send_block(spread_ref, out_ref, block):
    send(out_ref, lanes_of(block), combine(spread_ref[lanes_of(block), :].T))


def spread_rows(pot, spread_ref):
    for block in range(pot.shape[1] // LANES):
        spread_ref[lanes_of(block), :] = jnp.broadcast_to(pot[:, lanes_of(block)], (LANES, LANES)).T


def first_kernel(
    chips, cores, particles_hbm, weights_hbm, targets_hbm,
    score_ref, out_ref, weights_ref, half_ref,
    particles_ref, targets_ref, right_ref, points_sq_ref, spread_ref, sems,
):
    rows, size = particles_ref.shape
    width = targets_ref.shape[0]
    block = width // (chips * cores)
    scale = LOG2E / (EPS * size)
    copies = [
        pltpu.make_async_copy(targets_hbm, targets_ref, sems.at[0]),
        pltpu.make_async_copy(particles_hbm, particles_ref, sems.at[1]),
        pltpu.make_async_copy(weights_hbm, weights_ref, sems.at[2]),
    ]
    for copy in copies:
        copy.start()
    copies[0].wait()
    for tile in range(width // LANES):
        lanes = lanes_of(tile)
        parts, place = [], lanes.start
        while place < lanes.stop:
            core, chip = divmod(place // block, chips)
            count = min(lanes.stop, (place // block + 1) * block) - place
            start = (chip * cores + core) * block + place % block
            parts.append(targets_ref[start : start + count, :])
            place += count
        part = jnp.concatenate(parts, axis=0).T
        points_sq_ref[:, lanes] = jnp.sum(part * part, axis=0, keepdims=True) * scale
        high, low = split(part)
        for index, half in enumerate((high, low, high, low)):
            right_ref[index * size : (index + 1) * size, lanes] = half
    copies[1].wait()
    copies[2].wait()
    points_sq = points_sq_ref[...]
    step = 256

    def scores(index):
        part = slice(index * step, (index + 1) * step)
        source = particles_ref[part, :]
        source_sq = jnp.sum(source * source, axis=1, keepdims=True) * scale
        high, low = split(source * (2.0 * scale))
        left = jnp.concatenate([high, high, low, low], axis=1)
        cross = jnp.dot(left, right_ref[...], preferred_element_type=jnp.float32)
        cross = cross - source_sq - points_sq
        for core in range(cores):
            score_ref[core, part, :] = cross[:, core * width // cores : (core + 1) * width // cores]
        half_ref[:, part] = source.T.astype(jnp.bfloat16)

    def partials(index):
        for group in range(step // SUBS):
            row_group(score_ref, index * step + group * SUBS, None, spread_ref)
        for place in range(index * step // LANES, (index + 1) * step // LANES):
            send_block(spread_ref, out_ref, place)

    for index in range(rows // step):
        scores(index)
        if index:
            partials(index - 1)
    partials(rows // step - 1)


def row_kernel(log_count, score_ref, parts_ref, out_ref, spread_ref):
    cores, rows, width = score_ref.shape
    col_pot = -log_count - combine(received(parts_ref))
    pots = jnp.broadcast_to(col_pot, (SUBS, cores * width))
    pots = [pots[:, core * width : (core + 1) * width] for core in range(cores)]
    for block in range(rows // LANES):
        for group in range(LANES // SUBS):
            row_group(score_ref, block * LANES + group * SUBS, pots, spread_ref)
        send_block(spread_ref, out_ref, block)


def col_chunk(score_ref, spread_ref, step):
    base = step * CHUNK
    pots = [spread_ref[base + index * SUBS : base + (index + 1) * SUBS, :] for index in range(CHUNK // SUBS)]
    for tile in range(score_ref.shape[1] // LANES):
        yield tile, [
            score_ref[base + index * SUBS : base + (index + 1) * SUBS, lanes_of(tile)] + pot for index, pot in enumerate(pots)
        ]


def col_kernel(score_ref, parts_ref, weights_ref, out_ref, chunk_ref):
    cores, rows, width = score_ref.shape
    row_pot = weights_ref[...] * LOG2E - combine(received(parts_ref))
    for step in range(rows // CHUNK):
        spread = jnp.broadcast_to(row_pot[:, lanes_of(step)], (LANES, LANES)).T
        for core in range(cores):
            for tile in range(width // LANES):
                part = slice(step * CHUNK, (step + 1) * CHUNK)
                values = score_ref[core, part, lanes_of(tile)] + spread
                values = [values[index * SUBS : (index + 1) * SUBS] for index in range(CHUNK // SUBS)]
                lanes = lanes_of(core * width // LANES + tile)
                chunk_ref[step * SUBS : (step + 1) * SUBS, lanes] = lane_lse(values)
    send(out_ref, slice(0, cores * width), combine(chunk_ref[...]))


def half_sums(score_ref, half_ref, spread_ref, out_ref, plan_ref):
    rows, width = score_ref.shape
    size = half_ref.shape[0]
    tiles = width // LANES

    tops = [jnp.full((SUBS, LANES), LOWEST, jnp.float32) for _ in range(tiles)]
    for step in range(rows // CHUNK):
        for tile, values in col_chunk(score_ref, spread_ref, step):
            tops[tile] = jnp.maximum(tops[tile], tree(jnp.maximum, values))
    top = jnp.concatenate([jnp.max(top, axis=0, keepdims=True) for top in tops], axis=1)
    every = jnp.broadcast_to(top, (SUBS, width))
    totals = [jnp.zeros((SUBS, LANES), jnp.float32) for _ in range(tiles)]
    depth = 2 * CHUNK
    for part in range(rows // depth):
        for step in range(part * depth // CHUNK, (part + 1) * depth // CHUNK):
            for tile, values in col_chunk(score_ref, spread_ref, step):
                values = [jnp.exp2(value - every[:, lanes_of(tile)]) for value in values]
                totals[tile] = totals[tile] + tree(jnp.add, values)
                for index in range(0, len(values), 2):
                    base = step * CHUNK + index * SUBS
                    plan_ref[base : base + 2 * SUBS, lanes_of(tile)] = jnp.concatenate(
                        values[index : index + 2], axis=0
                    ).astype(jnp.bfloat16)
        inner = slice(part * depth, (part + 1) * depth)
        sums = jnp.dot(half_ref[:, inner], plan_ref[inner, :], preferred_element_type=jnp.float32)
        out_ref[:size, :] = out_ref[:size, :] + sums if part else sums
    total = jnp.concatenate([jnp.sum(total, axis=0, keepdims=True) for total in totals], axis=1)
    out_ref[size:, :] = jnp.concatenate([top, total, jnp.zeros((STATS - 2, width), jnp.float32)], axis=0)


def sibling_kernel(score_ref, parts_ref, weights_ref, half_ref, out_ref, spread_ref, plan_ref):
    row_pot = weights_ref[...] * LOG2E - combine(received(parts_ref))
    spread_rows(row_pot, spread_ref)
    half_sums(score_ref.at[1 - lax.axis_index("core")], half_ref, spread_ref, out_ref, plan_ref)


def own_kernel(score_ref, spread_ref, half_ref, out_ref, plan_ref):
    half_sums(score_ref.at[lax.axis_index("core")], half_ref, spread_ref, out_ref, plan_ref)


def join_kernel(own_ref, other_ref, out_ref):
    chips, block = out_ref.shape[0], out_ref.shape[1] - STATS
    size = own_ref.shape[0] - STATS
    tops = [ref[size : size + 1, :] for ref in (own_ref, other_ref)]
    top = jnp.maximum(*tops)
    own, other = (jnp.exp2(value - top) for value in tops)
    total = own_ref[size + 1 : size + 2, :] * own + other_ref[size + 1 : size + 2, :] * other
    sums = []
    for tile in range(own_ref.shape[1] // LANES):
        lanes = lanes_of(tile)
        sums.append((own_ref[:size, lanes] * own[:, lanes] + other_ref[:size, lanes] * other[:, lanes]).T)
    sums = jnp.concatenate(sums, axis=0)
    rest = jnp.zeros((1, LANES - block), jnp.float32)
    for chip in range(chips):
        part = slice(chip * block, (chip + 1) * block)
        out_ref[chip, :block, :] = sums[part]
        stats = [jnp.concatenate([row[:, part], rest], axis=1) for row in (top, total)]
        out_ref[chip, block:, :] = jnp.concatenate(stats + [jnp.zeros((STATS - 2, LANES), jnp.float32)], axis=0)


def final_kernel(blocks_ref, out_ref):
    chips, block = blocks_ref.shape[0], out_ref.shape[0]
    tops = [blocks_ref[chip, block : block + 1, :] for chip in range(chips)]
    top = tree(jnp.maximum, tops)
    shares = [jnp.exp2(value - top) for value in tops]
    total = tree(jnp.add, [blocks_ref[chip, block + 1 : block + 2, :] * share for chip, share in enumerate(shares)])
    scale = 1.0 / jnp.where(total > 0.0, total, 1.0)
    shares = jnp.concatenate([share * scale for share in shares], axis=0)
    shares = jnp.concatenate([shares, jnp.zeros((LANES - chips, LANES), jnp.float32)], axis=0).T
    out_ref[...] = tree(
        jnp.add, [blocks_ref[chip, :block, :] * shares[:block, chip : chip + 1] for chip in range(chips)]
    )


def exchange(sent, axis):
    return lax.all_to_all(sent, axis, 0, 0, tiled=True)


def per_device(particles, log_weights, targets):
    rows, size = particles.shape
    width = targets.shape[0]
    row_axes, col_axes = ("y", "core"), ("z", "x")
    chips, cores = lax.axis_size("y"), lax.axis_size("core")
    block = width // (chips * cores)
    log_count = math.log2(width * lax.axis_size(col_axes))
    params = pltpu.CompilerParams(vmem_limit_bytes=12 * 1024 * 1024)
    spread = pltpu.VMEM((rows, LANES), jnp.float32)
    to_cols = f32(lax.axis_size(col_axes), 1, rows)
    to_rows = f32(chips * cores, 1, width)

    score, local, weights, half = pl.pallas_call(
        lambda *refs: first_kernel(chips, cores, *refs),
        name="first_kernel",
        out_shape=(f32(cores, rows, width // cores), to_cols, f32(1, rows), jax.ShapeDtypeStruct((size, rows), jnp.bfloat16)),
        in_specs=[HBM] * 3,
        out_specs=(VMEM,) * 4,
        scratch_shapes=[
            pltpu.VMEM((rows, size), jnp.float32),
            pltpu.VMEM((width, size), jnp.float32),
            pltpu.VMEM((4 * size, width), jnp.bfloat16),
            pltpu.VMEM((1, width), jnp.float32),
            spread,
            pltpu.SemaphoreType.DMA((3,)),
        ],
        compiler_params=params,
    )(far(particles), far(log_weights.reshape(1, rows)), far(targets))
    for iteration in range(ITERS):
        if iteration:
            local = pl.pallas_call(
                lambda *refs: row_kernel(log_count, *refs),
                name="row_kernel",
                out_shape=to_cols,
                in_specs=[VMEM] * 2,
                out_specs=VMEM,
                scratch_shapes=[spread],
                compiler_params=params,
            )(score, parts)
        parts = exchange(local, col_axes)
        if iteration == ITERS - 1:
            break
        local = pl.pallas_call(
            col_kernel,
            out_shape=to_rows,
            in_specs=[VMEM] * 3,
            out_specs=VMEM,
            scratch_shapes=[pltpu.VMEM((rows // CHUNK * SUBS, width), jnp.float32)],
            compiler_params=params,
        )(score, parts, weights)
        parts = exchange(local, row_axes)
    part = f32(size + STATS, width // cores)
    plan = pltpu.VMEM((rows, width // cores), jnp.bfloat16)
    sent, spreads = pl.pallas_call(
        sibling_kernel,
        out_shape=(part, f32(rows, LANES)),
        in_specs=[VMEM] * 4,
        out_specs=(VMEM,) * 2,
        scratch_shapes=[plan],
        compiler_params=params,
    )(score, parts, weights, half)
    other = lax.ppermute(sent, "core", [(core, (core + 1) % cores) for core in range(cores)])
    own = pl.pallas_call(
        own_kernel,
        out_shape=part,
        in_specs=[VMEM] * 3,
        out_specs=VMEM,
        scratch_shapes=[plan],
        compiler_params=params,
        cost_estimate=pl.CostEstimate(
            flops=2 * rows * width * size // cores,
            bytes_accessed=4 * rows * width // cores,
            transcendentals=rows * width // cores,
        ),
    )(score, spreads, half)
    blocks = pl.pallas_call(
        join_kernel,
        out_shape=f32(chips, block + STATS, size),
        in_specs=[VMEM] * 2,
        out_specs=VMEM,
        compiler_params=params,
    )(own, other)
    blocks = exchange(blocks, "y")
    return pl.pallas_call(
        final_kernel,
        out_shape=f32(block, size),
        in_specs=[VMEM],
        out_specs=VMEM,
        compiler_params=params,
    )(blocks)


def solution(mesh):
    shape = dict(mesh.shape)
    row, col = shape["row"], shape["col"]
    devices = mesh.devices.reshape(row // 2, 2, col // 4, 4)
    parts = jax.sharding.Mesh(devices, ("y", "core", "z", "x"))
    rows, cols = ("y", "core"), ("z", "x")
    return jax.shard_map(
        per_device,
        mesh=parts,
        in_specs=(P(rows, None), P(rows), P(cols, None)),
        out_specs=P(cols + rows, None),
        check_vma=False,
    )
```

```python
import math

import jax
import jax.numpy as jnp
from jax import lax
from jax.experimental import pallas as pl
from jax.experimental.pallas import tpu as pltpu
from jax.sharding import PartitionSpec as P

ITERS = 3
EPS = 0.01
LOG2E = math.log2(math.e)
LANES = 128
SUBS = 8
CHUNK = 128
STATS = 8
LOWEST = -1e30
VMEM = pl.BlockSpec(memory_space=pltpu.VMEM)
HBM = pl.BlockSpec(memory_space=pltpu.HBM)


def far(x):
    return pltpu.with_memory_space_constraint(x, pltpu.HBM)


def f32(*shape):
    return jax.ShapeDtypeStruct(shape, jnp.float32)


def lanes_of(tile):
    return slice(tile * LANES, (tile + 1) * LANES)


def received(ref):
    return ref[...].reshape(ref.shape[0], ref.shape[2])


def send(out_ref, lanes, row):
    out_ref[:, :, lanes] = jnp.broadcast_to(row[None], (out_ref.shape[0], 1, row.shape[1]))


def combine(parts):
    top = jnp.max(parts, axis=0, keepdims=True)
    return top + jnp.log2(jnp.sum(jnp.exp2(parts - top), axis=0, keepdims=True))


def split(x):
    high = x.astype(jnp.bfloat16)
    low = (x - high.astype(jnp.float32)).astype(jnp.bfloat16)
    return high, low


def tree(op, values):
    while len(values) > 1:
        values = [op(*values[i : i + 2]) if i + 1 < len(values) else values[i] for i in range(0, len(values), 2)]
    return values[0]


def lane_lse(values):
    top = tree(jnp.maximum, values)
    return top + jnp.log2(tree(jnp.add, [jnp.exp2(value - top) for value in values]))


def row_group(score_ref, base, pots, spread_ref):
    rows = slice(base, base + SUBS)
    values = []
    for core in range(score_ref.shape[0]):
        for tile in range(score_ref.shape[2] // LANES):
            value = score_ref[core, rows, lanes_of(tile)]
            values.append(value if pots is None else value + pots[core][:, lanes_of(tile)])
    spread_ref[rows, :] = lane_lse(values)


def send_block(spread_ref, out_ref, block):
    send(out_ref, lanes_of(block), combine(spread_ref[lanes_of(block), :].T))


def spread_rows(pot, spread_ref):
    for block in range(pot.shape[1] // LANES):
        spread_ref[lanes_of(block), :] = jnp.broadcast_to(pot[:, lanes_of(block)], (LANES, LANES)).T


def first_kernel(
    chips, cores, particles_hbm, weights_hbm, targets_hbm,
    score_ref, out_ref, weights_ref, half_ref,
    particles_ref, targets_ref, right_ref, points_sq_ref, spread_ref, sems,
):
    rows, size = particles_ref.shape
    width = targets_ref.shape[0]
    block = width // (chips * cores)
    scale = LOG2E / (EPS * size)
    copies = [
        pltpu.make_async_copy(targets_hbm, targets_ref, sems.at[0]),
        pltpu.make_async_copy(particles_hbm, particles_ref, sems.at[1]),
        pltpu.make_async_copy(weights_hbm, weights_ref, sems.at[2]),
    ]
    for copy in copies:
        copy.start()
    copies[0].wait()
    for tile in range(width // LANES):
        lanes = lanes_of(tile)
        parts, place = [], lanes.start
        while place < lanes.stop:
            core, chip = divmod(place // block, chips)
            count = min(lanes.stop, (place // block + 1) * block) - place
            start = (chip * cores + core) * block + place % block
            parts.append(targets_ref[start : start + count, :])
            place += count
        part = jnp.concatenate(parts, axis=0).T
        points_sq_ref[:, lanes] = jnp.sum(part * part, axis=0, keepdims=True) * scale
        high, low = split(part)
        for index, half in enumerate((high, low, high, low)):
            right_ref[index * size : (index + 1) * size, lanes] = half
    copies[1].wait()
    copies[2].wait()
    points_sq = points_sq_ref[...]
    step = 256

    def scores(index):
        part = slice(index * step, (index + 1) * step)
        source = particles_ref[part, :]
        source_sq = jnp.sum(source * source, axis=1, keepdims=True) * scale
        high, low = split(source * (2.0 * scale))
        left = jnp.concatenate([high, high, low, low], axis=1)
        half_width = width // cores
        for core in range(cores):
            own = slice(core * half_width, (core + 1) * half_width)
            cross = jnp.dot(left, right_ref[:, own], preferred_element_type=jnp.float32)
            score_ref[core, part, :] = cross - source_sq - points_sq[:, own]
        half_ref[:, part] = source.T.astype(jnp.bfloat16)

    def partials(index):
        for group in range(step // SUBS):
            row_group(score_ref, index * step + group * SUBS, None, spread_ref)
        for place in range(index * step // LANES, (index + 1) * step // LANES):
            send_block(spread_ref, out_ref, place)

    for index in range(rows // step):
        scores(index)
        if index:
            partials(index - 1)
    partials(rows // step - 1)


def row_kernel(log_count, score_ref, parts_ref, out_ref, spread_ref):
    cores, rows, width = score_ref.shape
    col_pot = -log_count - combine(received(parts_ref))
    pots = jnp.broadcast_to(col_pot, (SUBS, cores * width))
    pots = [pots[:, core * width : (core + 1) * width] for core in range(cores)]
    for block in range(rows // LANES):
        for group in range(LANES // SUBS):
            row_group(score_ref, block * LANES + group * SUBS, pots, spread_ref)
        send_block(spread_ref, out_ref, block)


def col_chunk(score_ref, spread_ref, step):
    base = step * CHUNK
    pots = [spread_ref[base + index * SUBS : base + (index + 1) * SUBS, :] for index in range(CHUNK // SUBS)]
    for tile in range(score_ref.shape[1] // LANES):
        yield tile, [
            score_ref[base + index * SUBS : base + (index + 1) * SUBS, lanes_of(tile)] + pot for index, pot in enumerate(pots)
        ]


def col_kernel(score_ref, parts_ref, weights_ref, out_ref, chunk_ref):
    cores, rows, width = score_ref.shape
    row_pot = weights_ref[...] * LOG2E - combine(received(parts_ref))
    for step in range(rows // CHUNK):
        spread = jnp.broadcast_to(row_pot[:, lanes_of(step)], (LANES, LANES)).T
        for core in range(cores):
            for tile in range(width // LANES):
                part = slice(step * CHUNK, (step + 1) * CHUNK)
                values = score_ref[core, part, lanes_of(tile)] + spread
                values = [values[index * SUBS : (index + 1) * SUBS] for index in range(CHUNK // SUBS)]
                lanes = lanes_of(core * width // LANES + tile)
                chunk_ref[step * SUBS : (step + 1) * SUBS, lanes] = lane_lse(values)
    send(out_ref, slice(0, cores * width), combine(chunk_ref[...]))


def half_sums(score_ref, half_ref, spread_ref, out_ref, plan_ref):
    rows, width = score_ref.shape
    size = half_ref.shape[0]
    tiles = width // LANES

    tops = [jnp.full((SUBS, LANES), LOWEST, jnp.float32) for _ in range(tiles)]
    for step in range(rows // CHUNK):
        for tile, values in col_chunk(score_ref, spread_ref, step):
            tops[tile] = jnp.maximum(tops[tile], tree(jnp.maximum, values))
    top = jnp.concatenate([jnp.max(top, axis=0, keepdims=True) for top in tops], axis=1)
    every = jnp.broadcast_to(top, (SUBS, width))
    totals = [jnp.zeros((SUBS, LANES), jnp.float32) for _ in range(tiles)]
    depth = 2 * CHUNK
    for part in range(rows // depth):
        for step in range(part * depth // CHUNK, (part + 1) * depth // CHUNK):
            for tile, values in col_chunk(score_ref, spread_ref, step):
                values = [jnp.exp2(value - every[:, lanes_of(tile)]) for value in values]
                totals[tile] = totals[tile] + tree(jnp.add, values)
                for index in range(0, len(values), 2):
                    base = step * CHUNK + index * SUBS
                    plan_ref[base : base + 2 * SUBS, lanes_of(tile)] = jnp.concatenate(
                        values[index : index + 2], axis=0
                    ).astype(jnp.bfloat16)
        inner = slice(part * depth, (part + 1) * depth)
        sums = jnp.dot(half_ref[:, inner], plan_ref[inner, :], preferred_element_type=jnp.float32)
        out_ref[:size, :] = out_ref[:size, :] + sums if part else sums
    total = jnp.concatenate([jnp.sum(total, axis=0, keepdims=True) for total in totals], axis=1)
    out_ref[size:, :] = jnp.concatenate([top, total, jnp.zeros((STATS - 2, width), jnp.float32)], axis=0)


def sibling_kernel(score_ref, parts_ref, weights_ref, half_ref, out_ref, spread_ref, plan_ref):
    row_pot = weights_ref[...] * LOG2E - combine(received(parts_ref))
    spread_rows(row_pot, spread_ref)
    half_sums(score_ref.at[1 - lax.axis_index("core")], half_ref, spread_ref, out_ref, plan_ref)


def own_kernel(score_ref, spread_ref, half_ref, out_ref, plan_ref):
    half_sums(score_ref.at[lax.axis_index("core")], half_ref, spread_ref, out_ref, plan_ref)


def join_kernel(own_ref, other_ref, out_ref):
    chips, block = out_ref.shape[0], out_ref.shape[1] - STATS
    size = own_ref.shape[0] - STATS
    tops = [ref[size : size + 1, :] for ref in (own_ref, other_ref)]
    top = jnp.maximum(*tops)
    own, other = (jnp.exp2(value - top) for value in tops)
    total = own_ref[size + 1 : size + 2, :] * own + other_ref[size + 1 : size + 2, :] * other
    sums = []
    for tile in range(own_ref.shape[1] // LANES):
        lanes = lanes_of(tile)
        sums.append((own_ref[:size, lanes] * own[:, lanes] + other_ref[:size, lanes] * other[:, lanes]).T)
    sums = jnp.concatenate(sums, axis=0)
    rest = jnp.zeros((1, LANES - block), jnp.float32)
    for chip in range(chips):
        part = slice(chip * block, (chip + 1) * block)
        out_ref[chip, :block, :] = sums[part]
        stats = [jnp.concatenate([row[:, part], rest], axis=1) for row in (top, total)]
        out_ref[chip, block:, :] = jnp.concatenate(stats + [jnp.zeros((STATS - 2, LANES), jnp.float32)], axis=0)


def final_kernel(blocks_ref, out_ref):
    chips, block = blocks_ref.shape[0], out_ref.shape[0]
    tops = [blocks_ref[chip, block : block + 1, :] for chip in range(chips)]
    top = tree(jnp.maximum, tops)
    shares = [jnp.exp2(value - top) for value in tops]
    total = tree(jnp.add, [blocks_ref[chip, block + 1 : block + 2, :] * share for chip, share in enumerate(shares)])
    scale = 1.0 / jnp.where(total > 0.0, total, 1.0)
    shares = jnp.concatenate([share * scale for share in shares], axis=0)
    shares = jnp.concatenate([shares, jnp.zeros((LANES - chips, LANES), jnp.float32)], axis=0).T
    out_ref[...] = tree(
        jnp.add, [blocks_ref[chip, :block, :] * shares[:block, chip : chip + 1] for chip in range(chips)]
    )


def exchange(sent, axis):
    return lax.all_to_all(sent, axis, 0, 0, tiled=True)


def per_device(particles, log_weights, targets):
    rows, size = particles.shape
    width = targets.shape[0]
    row_axes, col_axes = ("y", "core"), ("z", "x")
    chips, cores = lax.axis_size("y"), lax.axis_size("core")
    block = width // (chips * cores)
    log_count = math.log2(width * lax.axis_size(col_axes))
    params = pltpu.CompilerParams(vmem_limit_bytes=12 * 1024 * 1024)
    spread = pltpu.VMEM((rows, LANES), jnp.float32)
    to_cols = f32(lax.axis_size(col_axes), 1, rows)
    to_rows = f32(chips * cores, 1, width)

    score, local, weights, half = pl.pallas_call(
        lambda *refs: first_kernel(chips, cores, *refs),
        name="first_kernel",
        out_shape=(f32(cores, rows, width // cores), to_cols, f32(1, rows), jax.ShapeDtypeStruct((size, rows), jnp.bfloat16)),
        in_specs=[HBM] * 3,
        out_specs=(VMEM,) * 4,
        scratch_shapes=[
            pltpu.VMEM((rows, size), jnp.float32),
            pltpu.VMEM((width, size), jnp.float32),
            pltpu.VMEM((4 * size, width), jnp.bfloat16),
            pltpu.VMEM((1, width), jnp.float32),
            spread,
            pltpu.SemaphoreType.DMA((3,)),
        ],
        compiler_params=params,
    )(far(particles), far(log_weights.reshape(1, rows)), far(targets))
    for iteration in range(ITERS):
        if iteration:
            local = pl.pallas_call(
                lambda *refs: row_kernel(log_count, *refs),
                name="row_kernel",
                out_shape=to_cols,
                in_specs=[VMEM] * 2,
                out_specs=VMEM,
                scratch_shapes=[spread],
                compiler_params=params,
            )(score, parts)
        parts = exchange(local, col_axes)
        if iteration == ITERS - 1:
            break
        local = pl.pallas_call(
            col_kernel,
            out_shape=to_rows,
            in_specs=[VMEM] * 3,
            out_specs=VMEM,
            scratch_shapes=[pltpu.VMEM((rows // CHUNK * SUBS, width), jnp.float32)],
            compiler_params=params,
        )(score, parts, weights)
        parts = exchange(local, row_axes)
    part = f32(size + STATS, width // cores)
    plan = pltpu.VMEM((rows, width // cores), jnp.bfloat16)
    sent, spreads = pl.pallas_call(
        sibling_kernel,
        out_shape=(part, f32(rows, LANES)),
        in_specs=[VMEM] * 4,
        out_specs=(VMEM,) * 2,
        scratch_shapes=[plan],
        compiler_params=params,
    )(score, parts, weights, half)
    other = lax.ppermute(sent, "core", [(core, (core + 1) % cores) for core in range(cores)])
    own = pl.pallas_call(
        own_kernel,
        out_shape=part,
        in_specs=[VMEM] * 3,
        out_specs=VMEM,
        scratch_shapes=[plan],
        compiler_params=params,
        cost_estimate=pl.CostEstimate(
            flops=2 * rows * width * size // cores,
            bytes_accessed=4 * rows * width // cores,
            transcendentals=rows * width // cores,
        ),
    )(score, spreads, half)
    blocks = pl.pallas_call(
        join_kernel,
        out_shape=f32(chips, block + STATS, size),
        in_specs=[VMEM] * 2,
        out_specs=VMEM,
        compiler_params=params,
    )(own, other)
    blocks = exchange(blocks, "y")
    return pl.pallas_call(
        final_kernel,
        out_shape=f32(block, size),
        in_specs=[VMEM],
        out_specs=VMEM,
        compiler_params=params,
    )(blocks)


def solution(mesh):
    shape = dict(mesh.shape)
    row, col = shape["row"], shape["col"]
    devices = mesh.devices.reshape(row // 2, 2, col // 4, 4)
    parts = jax.sharding.Mesh(devices, ("y", "core", "z", "x"))
    rows, cols = ("y", "core"), ("z", "x")
    return jax.shard_map(
        per_device,
        mesh=parts,
        in_specs=(P(rows, None), P(rows), P(cols, None)),
        out_specs=P(cols + rows, None),
        check_vma=False,
    )
```
